32 devices in a mesh: dp: 8 (over y, x, core), tensor: 4 (over z).
Axes of the slice: x: 2, y: 2, z: 4, core: 2. Of those that a mesh axis runs over, the one named last changes fastest.
Arguments:
- tokens: bfloat16 [4096, 4096], P(('dp', 'tensor')), may hold values from -120 to 120
- norm_gain: float32 [4096], replicated, may hold values from 0.5 to 1.5
- w_gate: bfloat16 [4096, 8192], P('dp', 'tensor'), may hold values from -0.09375 to 0.09375
- w_up: bfloat16 [4096, 8192], P('dp', 'tensor'), may hold values from -0.09375 to 0.09375
- probes: bfloat16 [4096, 2, 8192], P('dp', None, 'tensor'), may hold values from -0.09375 to 0.09375
- cotangent: bfloat16 [4096, 8192], P('dp', 'tensor'), may hold values from -6 to 6
Outputs:
- hvp: float32 [4096, 2, 8192], P('dp', None, 'tensor')
The draws below stay inside these ranges and needn't reach their ends.
All inputs are finite; a program needn't handle non-finite values.
Results may differ from the reference program's by a relative error of at most 0.014.
Values may be sent and summed in bfloat16 or wider, within the bound.
A program may use at most 128 MiB of HBM per device.

```python
import math
import jax
import jax.numpy as jnp
from jax import lax

D = 4096
FF = 8192
PROBES = 2
TOK_GROUP = 512
TOKENS = 4096
N_DP = 8


def draw_tokens(key, part):
    key_rows, key_cols, key_base = jax.random.split(key, 3)
    row_scale = jnp.exp(jax.random.uniform(key_rows, (TOKENS, 1), jnp.float32, 0.0, math.log(10.0)))
    col_scale = jnp.exp(jax.random.uniform(key_cols, (1, D), jnp.float32, 0.0, math.log(10.0)))
    base = jax.random.normal(key_base, (TOKENS, D), jnp.float32)
    base = jnp.clip(base, -4.0, 4.0)
    return (base * row_scale * col_scale * 0.3).astype(jnp.bfloat16)


def shard_levels(key, extent, pieces, smallest, top_value):
    loudness = 1.0
    for dim, shards_of in pieces:
        draws = jax.random.uniform(jax.random.fold_in(jax.random.fold_in(key, 6), dim), (shards_of,), jnp.float32, smallest / len(pieces), top_value / len(pieces))
        loudness = loudness * jnp.repeat(jnp.exp(draws), extent[dim] // shards_of).reshape((-1,) + (1,) * (len(extent) - 1 - dim))
    return loudness


def gaussian(stream_key, shape, spread, most, cuts=(), dtype=jnp.bfloat16):
    factor_of = shard_levels(stream_key, shape, cuts, -0.22, 0.18) if cuts else 1.0
    entries = jax.random.normal(stream_key, shape, jnp.float32) * spread * factor_of
    return jnp.minimum(jnp.maximum(entries, -most), most).astype(dtype)


def setup_inputs(seed: int = 0) -> dict:
    splits = jax.random.split(jax.random.key(seed), 7)
    return {
        "tokens": draw_tokens(jax.random.fold_in(splits[6], 71), 0),
        "norm_gain": jnp.clip(1.0 + 0.1 * jax.random.normal(splits[1], (D,), jnp.float32), 0.5, 1.5),
        "w_gate": gaussian(splits[2], (D, FF), D ** -0.5, 0.09375, ((0, 8), (1, 4))),
        "w_up": gaussian(splits[3], (D, FF), D ** -0.5, 0.09375, ((0, 8), (1, 4))),
        "probes": gaussian(splits[4], (D, PROBES, FF), D ** -0.5, 0.09375, ((0, 8), (2, 4))),
        "cotangent": gaussian(splits[5], (TOKENS, FF), 1.0, 6.0, ((0, 8), (1, 4))),
    }


def reference(tokens, norm_gain, w_gate, w_up, probes, cotangent):
    values = tokens.astype(jnp.float32)
    inverse = lax.rsqrt(lax.optimization_barrier(jnp.mean(values * values, axis=1, keepdims=True)) + 1e-05)
    normed = (values * inverse * norm_gain).astype(jnp.bfloat16)
    gate_pre = jnp.dot(normed, w_gate, preferred_element_type=jnp.float32)
    up_pre = jnp.dot(normed, w_up, preferred_element_type=jnp.float32)
    model_depth, probe_count, unit_count = probes.shape
    tangent = jnp.dot(normed, probes.reshape(model_depth, probe_count * unit_count), preferred_element_type=jnp.float32)
    tangent = tangent.reshape(normed.shape[0], probe_count, unit_count)
    logistic = jax.nn.sigmoid(gate_pre)
    curve = logistic * (1.0 - logistic) * (2.0 + gate_pre * (1.0 - 2.0 * logistic))
    weighting = cotangent.astype(jnp.float32) * curve * up_pre * (1.0 / math.sqrt(TOKENS))
    second = (weighting[:, None, :] * tangent).astype(jnp.bfloat16)
    grouped_rows = normed.reshape(N_DP, TOK_GROUP, model_depth)
    grouped_terms = second.reshape(N_DP, TOK_GROUP, probe_count * unit_count)

    def accumulate(totals, group_pair):
        partial_sum = jnp.dot(group_pair[0].T, group_pair[1], preferred_element_type=jnp.float32)
        rounded = lax.optimization_barrier(partial_sum.astype(jnp.bfloat16))
        return (totals + rounded.astype(jnp.float32), None)
    start_totals = jnp.zeros((model_depth, probe_count * unit_count), jnp.float32)
    totals, unused = lax.scan(accumulate, start_totals, (grouped_rows, grouped_terms))
    return totals.reshape(model_depth, probe_count, unit_count)
```

```python
import math

import jax
import jax.numpy as jnp
from jax import lax
from jax.sharding import PartitionSpec as P

LANES = 128
PARTS = (3, 3, 2)


def normalize(tokens, norm_gain):
    values = tokens.astype(jnp.float32)
    inverse = lax.rsqrt(jnp.mean(values * values, axis=1, keepdims=True) + 1e-05)
    return (values * inverse * norm_gain).astype(jnp.bfloat16)


def curvature(gate_pre):
    logistic = jax.nn.sigmoid(gate_pre)
    return logistic * (1.0 - logistic) * (2.0 + gate_pre * (1.0 - 2.0 * logistic))


def gather_weights(tokens, norm_gain, w_gate, w_up, probes, cotangent):
    normed = lax.all_gather(normalize(tokens, norm_gain), "tensor", axis=0, tiled=True)
    row_count = normed.shape[0]
    local_depth, probe_count, local_units = probes.shape
    probe_width = probe_count * local_units

    def project(shard_piece):
        return jnp.dot(normed, shard_piece, preferred_element_type=jnp.float32)

    gate_pre = project(lax.all_gather(w_gate, "dp", axis=0, tiled=True))
    up_pre = project(lax.all_gather(w_up, "dp", axis=0, tiled=True))
    shard_piece = lax.all_gather(probes, "dp", axis=0, tiled=True)
    tangent = project(shard_piece.reshape(shard_piece.shape[0], probe_width))
    scale_factor = 1.0 / math.sqrt(row_count * lax.axis_size("dp"))
    weighting = cotangent.astype(jnp.float32) * curvature(gate_pre) * up_pre * scale_factor
    second = (weighting[:, None, :] * tangent.reshape(row_count, probe_count, local_units)).astype(
        jnp.bfloat16
    )
    second = second.reshape(row_count, probe_width)
    result = lax.psum_scatter(
        lax.dot_general(
            normed, second, (((0,), (0,)), ((), ())), preferred_element_type=jnp.float32
        ).astype(jnp.bfloat16),
        "dp",
        scatter_dimension=0,
        tiled=True,
    ).astype(jnp.float32)
    return result.reshape(local_depth, probe_count, local_units)


def gather_tokens(tokens, norm_gain, w_gate, w_up, probes, cotangent):
    ways = lax.axis_size("dp")
    local_depth, probe_count, local_units = probes.shape
    depth = local_depth * ways
    units = local_units // ways
    group = cotangent.shape[0]

    def swap(blocks):
        return lax.all_to_all(jnp.stack(blocks), "dp", 0, 0, tiled=True)

    def columns(array, j, base=0):
        return array[:, base + j * units : base + (j + 1) * units]

    own = lax.all_gather(normalize(tokens, norm_gain), "tensor", axis=0, tiled=True)

    pair = swap(
        [jnp.concatenate([columns(w_gate, j), columns(w_up, j)], axis=1) for j in range(ways)]
    ).reshape(depth, 2 * units)
    cot = swap([columns(cotangent, j) for j in range(ways)])
    flat = probes.reshape(local_depth, probe_count * local_units)
    directions = swap(
        [
            jnp.concatenate(
                [columns(flat, j, p * local_units) for p in range(probe_count)], axis=1
            )
            for j in range(ways)
        ]
    ).reshape(depth, probe_count * units)

    scale_factor = 1.0 / math.sqrt(group * ways)
    total = None
    start = 0
    for part in PARTS:
        stop = start + group * part // sum(PARTS)
        gathered = lax.all_gather(own[start:stop], "dp", axis=0, tiled=True)
        if total is not None:
            gathered, total = lax.optimization_barrier((gathered, total))
        pre = jnp.dot(gathered, pair, preferred_element_type=jnp.float32)
        tangent = jnp.dot(gathered, directions, preferred_element_type=jnp.float32)
        here = cot[:, start:stop].reshape(-1, units).astype(jnp.float32)
        weighting = here * curvature(pre[:, :units]) * pre[:, units:] * scale_factor
        second = jnp.concatenate(
            [
                (weighting * columns(tangent, p)).astype(jnp.bfloat16)
                for p in range(probe_count)
            ],
            axis=1,
        )
        term = lax.dot_general(
            gathered, second, (((0,), (0,)), ((), ())), preferred_element_type=jnp.float32
        )
        total = term if total is None else total + term
        start = stop

    result = total.astype(jnp.bfloat16).reshape(ways, local_depth, probe_count * units)
    result = lax.all_to_all(result, "dp", 0, 0, tiled=True)
    flat = jnp.concatenate(
        [columns(result[j], p) for p in range(probe_count) for j in range(ways)], axis=1
    )
    return flat.reshape(local_depth, probe_count, local_units).astype(jnp.float32)


def per_device(tokens, norm_gain, w_gate, w_up, probes, cotangent):
    ways = lax.axis_size("dp")
    wide = w_gate.shape[1] % (ways * LANES) == 0 and cotangent.shape[0] % sum(PARTS) == 0
    plan = gather_tokens if wide else gather_weights
    return plan(tokens, norm_gain, w_gate, w_up, probes, cotangent)


def solution(mesh):
    in_specs = (
        P(("dp", "tensor"), None),
        P(),
        P("dp", "tensor"),
        P("dp", "tensor"),
        P("dp", None, "tensor"),
        P("dp", "tensor"),
    )
    out_specs = P("dp", None, "tensor")
    return jax.shard_map(
        per_device, mesh=mesh, in_specs=in_specs, out_specs=out_specs, check_vma=False
    )
```

```python
import math

import jax
import jax.numpy as jnp
from jax import lax
from jax.experimental import pallas as pl
from jax.sharding import PartitionSpec as P

LANES = 128
PARTS = (3, 3, 2)


def normalize(tokens, norm_gain):
    values = tokens.astype(jnp.float32)
    inverse = lax.rsqrt(jnp.mean(values * values, axis=1, keepdims=True) + 1e-05)
    return (values * inverse * norm_gain).astype(jnp.bfloat16)


def curvature(gate_pre):
    logistic = jax.nn.sigmoid(gate_pre)
    return logistic * (1.0 - logistic) * (2.0 + gate_pre * (1.0 - 2.0 * logistic))


def gather_weights(tokens, norm_gain, w_gate, w_up, probes, cotangent):
    normed = lax.all_gather(normalize(tokens, norm_gain), "tensor", axis=0, tiled=True)
    row_count = normed.shape[0]
    local_depth, probe_count, local_units = probes.shape
    probe_width = probe_count * local_units

    def project(shard_piece):
        return jnp.dot(normed, shard_piece, preferred_element_type=jnp.float32)

    gate_pre = project(lax.all_gather(w_gate, "dp", axis=0, tiled=True))
    up_pre = project(lax.all_gather(w_up, "dp", axis=0, tiled=True))
    shard_piece = lax.all_gather(probes, "dp", axis=0, tiled=True)
    tangent = project(shard_piece.reshape(shard_piece.shape[0], probe_width))
    scale_factor = 1.0 / math.sqrt(row_count * lax.axis_size("dp"))
    weighting = cotangent.astype(jnp.float32) * curvature(gate_pre) * up_pre * scale_factor
    second = (weighting[:, None, :] * tangent.reshape(row_count, probe_count, local_units)).astype(
        jnp.bfloat16
    )
    second = second.reshape(row_count, probe_width)
    result = lax.psum_scatter(
        lax.dot_general(
            normed, second, (((0,), (0,)), ((), ())), preferred_element_type=jnp.float32
        ).astype(jnp.bfloat16),
        "dp",
        scatter_dimension=0,
        tiled=True,
    ).astype(jnp.float32)
    return result.reshape(local_depth, probe_count, local_units)


def unpack(blocks, probe_count):
    ways, local_depth, width = blocks.shape
    units = width // probe_count
    rows = math.gcd(local_depth, 64)

    def kernel(blocks_ref, out_ref):
        for p in range(probe_count):
            for j in range(ways):
                piece = blocks_ref[j, :, p * units : (p + 1) * units]
                out_ref[:, p, j * units : (j + 1) * units] = piece.astype(jnp.float32)

    return pl.pallas_call(
        kernel,
        grid=(local_depth // rows,),
        in_specs=[pl.BlockSpec((ways, rows, width), lambda i: (0, i, 0))],
        out_specs=pl.BlockSpec((rows, probe_count, ways * units), lambda i: (i, 0, 0)),
        out_shape=jax.ShapeDtypeStruct((local_depth, probe_count, ways * units), jnp.float32),
        name="unpack",
    )(blocks)


def gather_tokens(tokens, norm_gain, w_gate, w_up, probes, cotangent):
    ways = lax.axis_size("dp")
    local_depth, probe_count, local_units = probes.shape
    depth = local_depth * ways
    units = local_units // ways
    group = cotangent.shape[0]

    def swap(blocks):
        return lax.all_to_all(jnp.stack(blocks), "dp", 0, 0, tiled=True)

    def columns(array, j, base=0):
        return array[:, base + j * units : base + (j + 1) * units]

    own = lax.all_gather(normalize(tokens, norm_gain), "tensor", axis=0, tiled=True)

    pair = swap(
        [jnp.concatenate([columns(w_gate, j), columns(w_up, j)], axis=1) for j in range(ways)]
    ).reshape(depth, 2 * units)
    cot = swap([columns(cotangent, j) for j in range(ways)])
    flat = probes.reshape(local_depth, probe_count * local_units)
    directions = swap(
        [
            jnp.concatenate(
                [columns(flat, j, p * local_units) for p in range(probe_count)], axis=1
            )
            for j in range(ways)
        ]
    ).reshape(depth, probe_count * units)

    own, pair, cot = lax.optimization_barrier((own, pair, cot))

    scale_factor = 1.0 / math.sqrt(group * ways)
    total = None
    start = 0
    for part in PARTS:
        stop = start + group * part // sum(PARTS)
        gathered = lax.all_gather(own[start:stop], "dp", axis=0, tiled=True)
        if total is not None:
            gathered, total = lax.optimization_barrier((gathered, total))
        pre = jnp.dot(gathered, pair, preferred_element_type=jnp.float32)
        tangent = jnp.dot(gathered, directions, preferred_element_type=jnp.float32)
        here = cot[:, start:stop].reshape(-1, units).astype(jnp.float32)
        weighting = here * curvature(pre[:, :units]) * pre[:, units:] * scale_factor
        second = jnp.concatenate(
            [
                (weighting * columns(tangent, p)).astype(jnp.bfloat16)
                for p in range(probe_count)
            ],
            axis=1,
        )
        term = lax.dot_general(
            gathered, second, (((0,), (0,)), ((), ())), preferred_element_type=jnp.float32
        )
        total = term if total is None else total + term
        start = stop

    result = total.astype(jnp.bfloat16).reshape(ways, local_depth, probe_count * units)
    result = lax.all_to_all(result, "dp", 0, 0, tiled=True)
    return unpack(result, probe_count)


def per_device(tokens, norm_gain, w_gate, w_up, probes, cotangent):
    ways = lax.axis_size("dp")
    wide = w_gate.shape[1] % (ways * LANES) == 0 and cotangent.shape[0] % sum(PARTS) == 0
    plan = gather_tokens if wide else gather_weights
    return plan(tokens, norm_gain, w_gate, w_up, probes, cotangent)


def solution(mesh):
    in_specs = (
        P(("dp", "tensor"), None),
        P(),
        P("dp", "tensor"),
        P("dp", "tensor"),
        P("dp", None, "tensor"),
        P("dp", "tensor"),
    )
    out_specs = P("dp", None, "tensor")
    return jax.shard_map(
        per_device, mesh=mesh, in_specs=in_specs, out_specs=out_specs, check_vma=False
    )
```

```python
import math

import jax
import jax.numpy as jnp
from jax import lax
from jax.experimental import pallas as pl
from jax.sharding import PartitionSpec as P

LANES = 128
PARTS = (5, 3)


def normalize(tokens, norm_gain):
    values = tokens.astype(jnp.float32)
    inverse = lax.rsqrt(jnp.mean(values * values, axis=1, keepdims=True) + 1e-05)
    return (values * inverse * norm_gain).astype(jnp.bfloat16)


def curvature(gate_pre):
    logistic = jax.nn.sigmoid(gate_pre)
    return logistic * (1.0 - logistic) * (2.0 + gate_pre * (1.0 - 2.0 * logistic))


def gather_weights(tokens, norm_gain, w_gate, w_up, probes, cotangent):
    normed = lax.all_gather(normalize(tokens, norm_gain), "tensor", axis=0, tiled=True)
    row_count = normed.shape[0]
    local_depth, probe_count, local_units = probes.shape
    probe_width = probe_count * local_units

    def project(shard_piece):
        return jnp.dot(normed, shard_piece, preferred_element_type=jnp.float32)

    gate_pre = project(lax.all_gather(w_gate, "dp", axis=0, tiled=True))
    up_pre = project(lax.all_gather(w_up, "dp", axis=0, tiled=True))
    shard_piece = lax.all_gather(probes, "dp", axis=0, tiled=True)
    tangent = project(shard_piece.reshape(shard_piece.shape[0], probe_width))
    scale_factor = 1.0 / math.sqrt(row_count * lax.axis_size("dp"))
    weighting = cotangent.astype(jnp.float32) * curvature(gate_pre) * up_pre * scale_factor
    second = (weighting[:, None, :] * tangent.reshape(row_count, probe_count, local_units)).astype(
        jnp.bfloat16
    )
    second = second.reshape(row_count, probe_width)
    result = lax.psum_scatter(
        lax.dot_general(
            normed, second, (((0,), (0,)), ((), ())), preferred_element_type=jnp.float32
        ).astype(jnp.bfloat16),
        "dp",
        scatter_dimension=0,
        tiled=True,
    ).astype(jnp.float32)
    return result.reshape(local_depth, probe_count, local_units)


def unpack(blocks, probe_count):
    ways, local_depth, width = blocks.shape
    units = width // probe_count
    rows = math.gcd(local_depth, 64)

    def kernel(blocks_ref, out_ref):
        for p in range(probe_count):
            for j in range(ways):
                piece = blocks_ref[j, :, p * units : (p + 1) * units]
                out_ref[:, p, j * units : (j + 1) * units] = piece.astype(jnp.float32)

    return pl.pallas_call(
        kernel,
        grid=(local_depth // rows,),
        in_specs=[pl.BlockSpec((ways, rows, width), lambda i: (0, i, 0))],
        out_specs=pl.BlockSpec((rows, probe_count, ways * units), lambda i: (i, 0, 0)),
        out_shape=jax.ShapeDtypeStruct((local_depth, probe_count, ways * units), jnp.float32),
        name="unpack",
    )(blocks)


def gather_tokens(tokens, norm_gain, w_gate, w_up, probes, cotangent):
    ways = lax.axis_size("dp")
    local_depth, probe_count, local_units = probes.shape
    depth = local_depth * ways
    units = local_units // ways
    group = cotangent.shape[0]

    def swap(blocks):
        return lax.all_to_all(jnp.stack(blocks), "dp", 0, 0, tiled=True)

    def columns(array, j, base=0):
        return array[:, base + j * units : base + (j + 1) * units]

    own = lax.all_gather(normalize(tokens, norm_gain), "tensor", axis=0, tiled=True)

    pair = swap(
        [jnp.concatenate([columns(w_gate, j), columns(w_up, j)], axis=1) for j in range(ways)]
    ).reshape(depth, 2 * units)
    cot = swap([columns(cotangent, j) for j in range(ways)])
    flat = probes.reshape(local_depth, probe_count * local_units)
    directions = swap(
        [
            jnp.concatenate(
                [columns(flat, j, p * local_units) for p in range(probe_count)], axis=1
            )
            for j in range(ways)
        ]
    ).reshape(depth, probe_count * units)

    own, pair, cot = lax.optimization_barrier((own, pair, cot))

    scale_factor = 1.0 / math.sqrt(group * ways)
    total = None
    start = 0
    for part in PARTS:
        stop = start + group * part // sum(PARTS)
        gathered = lax.all_gather(own[start:stop], "dp", axis=0, tiled=True)
        if total is not None:
            gathered, total = lax.optimization_barrier((gathered, total))
        pre = jnp.dot(gathered, pair, preferred_element_type=jnp.float32)
        tangent = jnp.dot(gathered, directions, preferred_element_type=jnp.float32)
        here = cot[:, start:stop].reshape(-1, units).astype(jnp.float32)
        weighting = here * curvature(pre[:, :units]) * pre[:, units:] * scale_factor
        second = jnp.concatenate(
            [
                (weighting * columns(tangent, p)).astype(jnp.bfloat16)
                for p in range(probe_count)
            ],
            axis=1,
        )
        term = lax.dot_general(
            gathered, second, (((0,), (0,)), ((), ())), preferred_element_type=jnp.float32
        )
        total = term if total is None else total + term
        start = stop

    result = total.astype(jnp.bfloat16).reshape(ways, local_depth, probe_count * units)
    result = lax.all_to_all(result, "dp", 0, 0, tiled=True)
    return unpack(result, probe_count)


def per_device(tokens, norm_gain, w_gate, w_up, probes, cotangent):
    ways = lax.axis_size("dp")
    wide = w_gate.shape[1] % (ways * LANES) == 0 and cotangent.shape[0] % sum(PARTS) == 0
    plan = gather_tokens if wide else gather_weights
    return plan(tokens, norm_gain, w_gate, w_up, probes, cotangent)


def solution(mesh):
    in_specs = (
        P(("dp", "tensor"), None),
        P(),
        P("dp", "tensor"),
        P("dp", "tensor"),
        P("dp", None, "tensor"),
        P("dp", "tensor"),
    )
    out_specs = P("dp", None, "tensor")
    return jax.shard_map(
        per_device, mesh=mesh, in_specs=in_specs, out_specs=out_specs, check_vma=False
    )
```
